32 devices in a mesh: dom: 16 (over z, x, core), feat: 2 (over y).
Axes of the slice: x: 2, y: 2, z: 4, core: 2. Of those that a mesh axis runs over, the one named last changes fastest.
Arguments:
- features: bfloat16 [65536, 1024], P('dom', 'feat'), may hold values from -6 to 6
- w_self: bfloat16 [1024, 256], P('feat'), may hold values from -0.1875 to 0.1875
- w_neigh: bfloat16 [1024, 256], P('feat'), may hold values from -0.1875 to 0.1875
- hidden_bias: float32 [256], replicated, may hold values from -3 to 3
- edge_tiles: bfloat16 [16, 102, 128, 128], P('dom'), may hold values from 0 to 0.099609375
- tile_dst: int32 [16, 102], P('dom'), may hold values from 0 to 31, as said below
- tile_src: int32 [16, 102], P('dom'), may hold values from 0 to 47, as said below
- tile_count: int32 [16], P('dom'), may hold values from 12 to 102, as said below
- bound_rows: int32 [16, 256], P('dom'), may hold values from 0 to 4095, as said below
- send_pick: int32 [16, 16, 128], P('dom'), may hold values from 0 to 255, as said below
- cotangent: bfloat16 [65536, 256], P(('dom', 'feat')), may hold values from -0.0234375 to 0.0234375
Outputs:
- hidden: bfloat16 [65536, 256], P(('dom', 'feat'))
- grad_self: bfloat16 [1024, 256], P('feat')
- grad_neigh: bfloat16 [1024, 256], P('feat')
- grad_bias: float32 [256], replicated
The draws below stay inside these ranges and needn't reach their ends.
Inputs may be any that keep to these rules, and one draw needn't show every extreme that they name: Within a partition the pairs (tile_dst, tile_src) of its 102 slots are distinct. `tile_src`: A source block below 32 is a row tile of the partition itself; block 32 + q is the block received from partition q. Slots from tile_count[p] on are unused. Some partition uses all 102 slots. `bound_rows`: distinct within each partition. Each list send_pick[p, q] has no repeats.
All inputs are finite; a program needn't handle non-finite values.
Results may differ from the reference program's by a relative error of at most 0.009.
The reference program's roundings to bfloat16 on the way (of `received`, `source`, `aggregated` and `pre_grad`) count: a program that leaves them out, or rounds other values in their place, can miss the bound.
Values may be sent and summed in bfloat16 or wider, within the bound.
A program may use at most 128 MiB of HBM per device.

```python
import jax
import jax.numpy as jnp
from jax import lax

F = 1024
H = 256
TILE = 128
NPD = 4096
UB = 256
ET = 102
PARTS_SIZE = 16
NODES = 65536


def tile_lists(key):
    dest_tiles = NPD // TILE
    blocks = dest_tiles + PARTS_SIZE
    pair_count = dest_tiles * blocks
    subkeys = jax.random.split(jax.random.fold_in(key, 11), PARTS_SIZE)

    def pick_pairs(subkey):
        return jax.random.permutation(subkey, pair_count)[:ET]
    chosen = jax.vmap(pick_pairs)(subkeys)
    return ((chosen // blocks).astype(jnp.int32), (chosen % blocks).astype(jnp.int32))


def draw_tile_dst(key, part):
    return tile_lists(key)[0]


def draw_tile_src(key, part):
    return tile_lists(key)[1]


def draw_tile_count(key, part):
    raw_draw = jax.random.randint(jax.random.fold_in(key, 23), (PARTS_SIZE,), 0, ET + 1)
    counts = jnp.maximum(ET // 8, raw_draw * raw_draw // ET)
    fullest = jax.random.randint(jax.random.fold_in(key, 29), (), 0, PARTS_SIZE)
    return jnp.where(jnp.arange(PARTS_SIZE) == fullest, ET, counts).astype(jnp.int32)


def draw_bound_rows(key, part):
    subkeys = jax.random.split(jax.random.fold_in(key, 31), PARTS_SIZE)

    def take_boundary(subkey):
        return jax.random.permutation(subkey, NPD)[:UB]
    return jax.vmap(take_boundary)(subkeys).astype(jnp.int32)


def draw_send_pick(key, part):
    subkeys = jax.random.split(jax.random.fold_in(key, 37), PARTS_SIZE * PARTS_SIZE)

    def take_picks(subkey):
        return jax.random.permutation(subkey, UB)[:TILE]
    return jax.vmap(take_picks)(subkeys).reshape(PARTS_SIZE, PARTS_SIZE, TILE).astype(jnp.int32)


def shard_levels(own_key, extent, shards, low, largest):
    level, own = 1.0, jax.random.fold_in(own_key, 6)
    for dim, blocks in shards:
        heights = jnp.exp(jax.random.uniform(jax.random.fold_in(own, dim), (blocks,), jnp.float32, low / len(shards), largest / len(shards)))
        level = level * jnp.repeat(heights, extent[dim] // blocks).reshape([-1 if axis == dim else 1 for axis in range(len(extent))])
    return level


def gaussian(rng, shape, spread, bound, cuts=(), held_as=jnp.bfloat16):
    factor_of = shard_levels(rng, shape, cuts, -0.22, 0.18) if cuts else 1.0
    array = jax.random.normal(rng, shape, jnp.float32) * spread * factor_of
    return jnp.minimum(jnp.maximum(array, -bound), bound).astype(held_as)


def setup_inputs(seed: int = 0) -> dict:
    seeds = jax.random.split(jax.random.key(seed), 12)
    features = gaussian(seeds[0], (NODES, F), 1.0, 6.0, ((0, 16), (1, 2)))
    w_self = gaussian(seeds[1], (F, H), F ** -0.5, 0.1875, ((0, 2),))
    w_neigh = gaussian(seeds[2], (F, H), F ** -0.5, 0.1875, ((0, 2),))
    hidden_bias = gaussian(seeds[3], (H,), 0.5, 3.0, (), jnp.float32)
    edge_tiles = jnp.clip(0.099609375 * jax.random.uniform(seeds[4], (PARTS_SIZE, ET, TILE, TILE), jnp.float32) ** shard_levels(seeds[4], (PARTS_SIZE, ET, TILE, TILE), ((0, 16),), -0.2, 0.2), 0.0, 0.099609375).astype(jnp.bfloat16)
    tile_dst = draw_tile_dst(jax.random.fold_in(seeds[11], 71), 0)
    tile_src = draw_tile_src(jax.random.fold_in(seeds[11], 71), 0)
    tile_count = draw_tile_count(jax.random.fold_in(seeds[11], 71), 0)
    bound_rows = draw_bound_rows(jax.random.fold_in(seeds[11], 71), 0)
    send_pick = draw_send_pick(jax.random.fold_in(seeds[11], 71), 0)
    cotangent = gaussian(seeds[10], (NODES, H), (1.0 / NODES ** 0.5), 0.0234375, ((0, 32),))
    return {"features": features, "w_self": w_self, "w_neigh": w_neigh, "hidden_bias": hidden_bias, "edge_tiles": edge_tiles, "tile_dst": tile_dst, "tile_src": tile_src, "tile_count": tile_count, "bound_rows": bound_rows, "send_pick": send_pick, "cotangent": cotangent}


def reference(features, w_self, w_neigh, hidden_bias, edge_tiles, tile_dst, tile_src, tile_count, bound_rows, send_pick, cotangent):
    dest_tiles = NPD // TILE
    part_offsets = (jnp.arange(PARTS_SIZE, dtype=jnp.int32) * NPD)[:, None]
    weights = jnp.concatenate([w_self, w_neigh], 0)
    dest_ids = jnp.arange(dest_tiles, dtype=jnp.int32)[:, None]
    slot_ids = jnp.arange(ET, dtype=jnp.int32)

    def one_part(totals, part_index):
        local_rows = lax.dynamic_slice_in_dim(features, part_index * NPD, NPD, 0)
        pick_rows = lax.dynamic_index_in_dim(send_pick, part_index, 1, keepdims=False)
        global_ids = (jnp.take_along_axis(bound_rows, pick_rows, axis=1) + part_offsets).reshape(-1)
        received = jnp.take(features, global_ids, axis=0)
        source = jnp.concatenate([local_rows, received], 0).reshape(-1, TILE, F)
        picked = jnp.take(source, tile_src[part_index], axis=0)
        products = jnp.einsum("etc,ecf->etf", edge_tiles[part_index].astype(jnp.float32), picked.astype(jnp.float32), precision=lax.Precision.HIGHEST)
        live_slots = (slot_ids < tile_count[part_index]).astype(jnp.float32)
        onehot = (tile_dst[part_index][None, :] == dest_ids).astype(jnp.float32) * live_slots[None, :]
        aggregated = jnp.einsum("de,etf->dtf", onehot, products, precision=lax.Precision.HIGHEST).reshape(NPD, F).astype(jnp.bfloat16)
        stacked = jnp.concatenate([local_rows, aggregated], 1)
        preact = jnp.dot(stacked, weights, preferred_element_type=jnp.float32) + hidden_bias
        hidden = jnp.maximum(preact, 0.0).astype(jnp.bfloat16)
        grad_rows = lax.dynamic_slice_in_dim(cotangent, part_index * NPD, NPD, 0)
        pre_grad = jnp.where(preact > 0.0, grad_rows, jnp.zeros_like(grad_rows))
        gradients = jnp.dot(stacked.T, pre_grad, preferred_element_type=jnp.float32)
        bias_grad = jnp.sum(pre_grad.astype(jnp.float32), 0)
        return (totals[0] + gradients, totals[1] + bias_grad), hidden

    start_totals = (jnp.zeros((2 * F, H), jnp.float32), jnp.zeros((H,), jnp.float32))
    totals, hidden = lax.scan(one_part, start_totals, jnp.arange(PARTS_SIZE, dtype=jnp.int32))
    gradients, bias_grad = totals
    hidden = hidden.reshape(NODES, H)
    return hidden, gradients[:F].astype(jnp.bfloat16), gradients[F:].astype(jnp.bfloat16), bias_grad
```

```python
import functools

import jax
import jax.numpy as jnp
from jax import lax
from jax.experimental import pallas as pl
from jax.experimental.pallas import tpu as pltpu
from jax.sharding import PartitionSpec as P

MESH = pl.DeviceIdType.MESH
F32 = jnp.float32
BF16 = jnp.bfloat16
VMEM = pl.BlockSpec(memory_space=pltpu.VMEM)
SMEM = pl.BlockSpec(memory_space=pltpu.SMEM)
ANY = pl.BlockSpec(memory_space=pl.ANY)
TN = (((0,), (0,)), ((), ()))


def boundary_kernel(n, feat_ref, bound_ref, pick_ref, out_ref, blocks, send, recv, side_send, side_recv):
    chips = n // 2
    turn = chips // 2
    full = chips // 2 - 1
    ub = bound_ref.shape[1]
    width = feat_ref.shape[1]
    pick = pick_ref.shape[1]
    half_rows = ub // 2
    parts = ((0, half_rows), (half_rows, ub - half_rows + n))

    me = lax.axis_index("dom")
    core = me % 2
    chip = me // 2
    col = chip % 2
    row = chip // 2
    place = (1 - col) * row + col * (chips - 1 - row)

    def dom_of(position, which):
        position = (position + 2 * chips) % chips
        up = position // turn
        at = (1 - up) * 2 * position + up * (2 * (chips - 1 - position) + 1)
        return at * 2 + which

    ahead = dom_of(place + 1, core)
    behind = dom_of(place - 1, core)
    sibling = me + 1 - 2 * core

    barrier = pltpu.get_barrier_semaphore()
    for other in (ahead, behind, sibling):
        pl.semaphore_signal(barrier, inc=1, device_id={"dom": other}, device_id_type=MESH)

    nodes = feat_ref.shape[0]
    depth = min(512, nodes)
    wanted = bound_ref[0:1, :]

    def add_rows(k, total):
        ids = lax.broadcasted_iota(jnp.int32, (depth, ub), 0) + k * depth
        hot = jnp.where(ids == wanted, 1.0, 0.0).astype(BF16)
        rows = feat_ref[pl.ds(pl.multiple_of(k * depth, depth), depth), :]
        return total + lax.dot_general(hot, rows, TN, preferred_element_type=F32)

    total = lax.fori_loop(0, nodes // depth, add_rows, jnp.zeros((ub, width), F32))
    blocks[me, 0:ub, :] = total.astype(BF16)
    blocks[me, ub : ub + n, 0:pick] = pick_ref[...]
    if width > pick:
        blocks[me, ub : ub + n, pick:width] = jnp.zeros((n, width - pick), BF16)
    pl.semaphore_wait(barrier, 3)

    def hop(way, step, h):
        source = place - step if way == 0 else place + step
        owner = dom_of(source, core)
        at = blocks.at[owner, pl.ds(parts[h][0], parts[h][1])]
        return pltpu.make_async_remote_copy(
            src_ref=at,
            dst_ref=at,
            send_sem=send.at[way, step, h],
            recv_sem=recv.at[way, step, h],
            device_id={"dom": ahead if way == 0 else behind},
            device_id_type=MESH,
        )

    def aside(i, owner):
        return pltpu.make_async_remote_copy(
            src_ref=blocks.at[owner],
            dst_ref=blocks.at[owner],
            send_sem=side_send.at[i],
            recv_sem=side_recv.at[i],
            device_id={"dom": sibling},
            device_id_type=MESH,
        )

    def take(owner):
        table = blocks[owner, ub : ub + n, 0:pick].astype(F32)
        rows = lax.broadcasted_iota(jnp.int32, (n, pick), 0)
        mine = jnp.sum(jnp.where(rows == me, table, 0.0), axis=0, keepdims=True)
        ids = lax.broadcasted_iota(jnp.int32, (ub, pick), 0).astype(F32)
        hot = jnp.where(ids == mine, 1.0, 0.0).astype(BF16)
        got = lax.dot_general(hot, blocks[owner, 0:ub, :], TN, preferred_element_type=F32)
        out_ref[owner] = got.astype(BF16)

    started = []
    sides = []
    side_seen = 0

    def arrived(position):
        i = len(sides)
        copy = aside(i, dom_of(position, core))
        copy.start()
        sides.append((copy, position))

    for step in range(full + 1):
        for h in (0, 1):
            for way in (0, 1):
                if step > 0:
                    hop(way, step - 1, h).wait_recv()
                if step < full or h == way:
                    copy = hop(way, step, h)
                    copy.start()
                    started.append(copy)
        if step == 0:
            arrived(place)
            take(me)
        else:
            for position in (place - step, place + step):
                arrived(position)
                take(dom_of(position, core))
            while side_seen < len(sides) - 2:
                copy, position = sides[side_seen]
                copy.wait_recv()
                take(dom_of(position, 1 - core))
                side_seen += 1
    hop(0, full, 0).wait_recv()
    hop(1, full, 1).wait_recv()
    arrived(place + full + 1)
    take(dom_of(place + full + 1, core))
    while side_seen < len(sides):
        copy, position = sides[side_seen]
        copy.wait_recv()
        take(dom_of(position, 1 - core))
        side_seen += 1
    for copy in started:
        copy.wait_send()
    for copy, _ in sides:
        copy.wait_send()


def received_blocks(n, features, bound_rows, send_pick):
    width = features.shape[1]
    ub = bound_rows.shape[1]
    pick = send_pick.shape[1]
    steps = n // 4
    return pl.pallas_call(
        functools.partial(boundary_kernel, n),
        out_shape=jax.ShapeDtypeStruct((n, pick, width), BF16),
        in_specs=[VMEM] * 3,
        out_specs=VMEM,
        scratch_shapes=[
            pltpu.VMEM((n, ub + n, width), BF16),
            pltpu.SemaphoreType.DMA((2, steps, 2)),
            pltpu.SemaphoreType.DMA((2, steps, 2)),
            pltpu.SemaphoreType.DMA((n // 2,)),
            pltpu.SemaphoreType.DMA((n // 2,)),
        ],
        compiler_params=pltpu.CompilerParams(
            collective_id=0, has_side_effects=True, vmem_limit_bytes=40 * 2**20
        ),
    )(features, bound_rows, send_pick.astype(BF16))


def tile_kernel(group, dst_ref, src_ref, count_ref, feat_ref, recv_ref, tiles_ref, out_ref, source, total, sems):
    tile = tiles_ref.shape[1]
    nodes = feat_ref.shape[0]
    copies = (
        pltpu.make_async_copy(feat_ref, source.at[pl.ds(0, nodes)], sems.at[0]),
        pltpu.make_async_copy(recv_ref, source.at[pl.ds(nodes, recv_ref.shape[0])], sems.at[1]),
    )
    for copy in copies:
        copy.start()
    total[...] = jnp.zeros_like(total)
    for copy in copies:
        copy.wait()
    count = count_ref[0]

    def slots(g, carry):
        products = []
        for u in range(group):
            e = g * group + u
            block = source[pl.ds(pl.multiple_of(src_ref[0, e] * tile, tile), tile), :]
            product = jnp.dot(tiles_ref[e], block, preferred_element_type=F32)
            products.append(jnp.where(e < count, product, 0.0))
        for u in range(group):
            e = g * group + u
            at = pl.ds(pl.multiple_of(dst_ref[0, e] * tile, tile), tile)
            total[at, :] += products[u]
        return carry

    lax.fori_loop(0, (count + group - 1) // group, slots, 0)
    out_ref[...] = total[...].astype(BF16)


def aggregate(features, received, edge_tiles, tile_dst, tile_src, tile_count):
    nodes, width = features.shape
    slots = edge_tiles.shape[0]
    group = next(g for g in (3, 2, 1) if slots % g == 0)
    rows = received.shape[0]
    return pl.pallas_call(
        functools.partial(tile_kernel, group),
        out_shape=jax.ShapeDtypeStruct((nodes, width), BF16),
        in_specs=[SMEM, SMEM, SMEM, ANY, ANY, VMEM],
        out_specs=VMEM,
        scratch_shapes=[
            pltpu.VMEM((nodes + rows, width), BF16),
            pltpu.VMEM((nodes, width), F32),
            pltpu.SemaphoreType.DMA((2,)),
        ],
        compiler_params=pltpu.CompilerParams(vmem_limit_bytes=40 * 2**20),
    )(tile_dst, tile_src, tile_count, features, received, edge_tiles)


def halving_plan(n, rows):
    plan = []
    length = rows
    bit = 1
    while bit < n:
        halve = length % 32 == 0
        if halve:
            length //= 2
        plan.append((bit, halve, length))
        bit *= 2
    return plan


def layer_kernel(
    n, nf, plan, chunk,
    feat_ref, agg_ref, ws_ref, wn_ref, bias_ref, cot_ref,
    hidden_ref, gs_ref, gn_ref, gb_ref,
    outgoing, incoming, own, grads, total, sums, result, halves, small,
    psend, precv, gsend, grecv, hsend, hrecv, bsend, brecv, asend, arecv,
):
    me = lax.axis_index("dom")
    f = lax.axis_index("feat")
    owned = cot_ref.shape[0]
    width = feat_ref.shape[1]
    chunks = owned // chunk
    partners = []
    for bit, _, _ in plan:
        side = (me // bit) % 2
        partners.append((me + bit - 2 * bit * side, side))
    peers = [(f + k) % nf for k in range(1, nf)]

    barrier = pltpu.get_barrier_semaphore()
    for peer in peers:
        pl.semaphore_signal(barrier, inc=1, device_id={"feat": peer}, device_id_type=MESH)
    for partner, _ in partners:
        pl.semaphore_signal(barrier, inc=1, device_id={"dom": partner}, device_id_type=MESH)
    pl.semaphore_wait(barrier, nf - 1 + len(plan))

    def at_rows(owner, j):
        return pl.ds(pl.multiple_of(owner * owned + j * chunk, chunk), chunk)

    def partial(owner, j):
        rows = at_rows(owner, j)
        return jnp.dot(feat_ref[rows, :], ws_ref[...], preferred_element_type=F32) + jnp.dot(
            agg_ref[rows, :], wn_ref[...], preferred_element_type=F32
        )

    def inside(j):
        return pl.ds(pl.multiple_of(j * chunk, chunk), chunk)

    def partial_copy(k, j):
        return pltpu.make_async_remote_copy(
            src_ref=outgoing.at[k, inside(j)],
            dst_ref=incoming.at[k, inside(j)],
            send_sem=psend.at[k, j],
            recv_sem=precv.at[k, j],
            device_id={"feat": peers[k]},
            device_id_type=MESH,
        )

    def grad_copy(k, j):
        rows = at_rows(f, j)
        return pltpu.make_async_remote_copy(
            src_ref=grads.at[rows],
            dst_ref=grads.at[rows],
            send_sem=gsend.at[k, j],
            recv_sem=grecv.at[k, j],
            device_id={"feat": peers[k]},
            device_id_type=MESH,
        )

    def send_partials(j, carry):
        for k in range(nf - 1):
            outgoing[k, inside(j), :] = partial(peers[k], j).astype(outgoing.dtype)
            partial_copy(k, j).start()
        return carry

    lax.fori_loop(0, chunks, send_partials, 0)

    def own_partials(j, carry):
        own[inside(j), :] = partial(f, j)
        return carry

    lax.fori_loop(0, chunks, own_partials, 0)
    total[...] = jnp.zeros_like(total)

    def add_grads(owner, j):
        rows = at_rows(owner, j)
        block = grads[rows, :]
        total[0:width, :] += lax.dot_general(feat_ref[rows, :], block, TN, preferred_element_type=F32)
        total[width : 2 * width, :] += lax.dot_general(
            agg_ref[rows, :], block, TN, preferred_element_type=F32
        )
        wide = block.astype(F32).reshape(chunk // 8, 8, block.shape[1])
        sums[owner * chunks + j] = jnp.sum(wide, axis=0)

    def finish_rows(j, carry):
        for k in range(nf - 1):
            partial_copy(k, j).wait_recv()
        preact = own[inside(j), :]
        for k in range(nf - 1):
            preact = preact + incoming[k, inside(j), :].astype(F32)
        preact = preact + bias_ref[...]
        hidden_ref[inside(j), :] = jnp.maximum(preact, 0.0).astype(BF16)
        grads[at_rows(f, j), :] = jnp.where(preact > 0.0, cot_ref[inside(j), :].astype(F32), 0.0).astype(BF16)
        for k in range(nf - 1):
            grad_copy(k, j).start()
        add_grads(f, j)
        return carry

    lax.fori_loop(0, chunks, finish_rows, 0)

    def other_rows(j, carry):
        for k in range(nf - 1):
            owner = (f + nf - 1 - k) % nf
            grad_copy(k, j).wait_recv()
            add_grads(owner, j)
        return carry

    lax.fori_loop(0, chunks, other_rows, 0)

    def add_sums(i, acc):
        return acc + sums[i]

    bias_sum = lax.fori_loop(0, nf * chunks, add_sums, jnp.zeros(sums.shape[1:], F32))
    bias_sum = jnp.broadcast_to(jnp.sum(bias_sum, axis=0, keepdims=True), bias_sum.shape)

    started = []
    base = 0
    bases = []
    slot = 0
    for s, (bit, halve, length) in enumerate(plan):
        partner, side = partners[s]
        bases.append(base)
        if halve:
            keep = base + side * length
            give = base + (1 - side) * length
        else:
            keep = give = base
        keep_rows = pl.ds(pl.multiple_of(keep, 16), length)
        give_rows = pl.ds(pl.multiple_of(give, 16), length)
        small[2 * s] = bias_sum
        if not halve:
            result_rows = pl.ds(slot, length)
        copy = pltpu.make_async_remote_copy(
            src_ref=total.at[give_rows] if halve else halves[s][1],
            dst_ref=halves[s][0],
            send_sem=hsend.at[s],
            recv_sem=hrecv.at[s],
            device_id={"dom": partner},
            device_id_type=MESH,
        )
        if not halve:
            halves[s][1][...] = total[give_rows, :]
        copy.start()
        tiny = pltpu.make_async_remote_copy(
            src_ref=small.at[2 * s],
            dst_ref=small.at[2 * s + 1],
            send_sem=bsend.at[s],
            recv_sem=brecv.at[s],
            device_id={"dom": partner},
            device_id_type=MESH,
        )
        tiny.start()
        started += [copy, tiny]
        copy.wait_recv()
        total[keep_rows, :] += halves[s][0][...]
        tiny.wait_recv()
        bias_sum = bias_sum + small[2 * s + 1]
        base = keep
    last = plan[-1][2]
    rows = pl.ds(pl.multiple_of(base, 16), last)
    result[rows, :] = total[rows, :].astype(BF16)
    gb_ref[...] = bias_sum
    held = last
    for s in range(len(plan) - 1, -1, -1):
        bit, halve, length = plan[s]
        if not halve:
            continue
        partner, side = partners[s]
        mine = pl.ds(pl.multiple_of(bases[s] + side * length, 16), length)
        copy = pltpu.make_async_remote_copy(
            src_ref=result.at[mine],
            dst_ref=result.at[mine],
            send_sem=asend.at[s],
            recv_sem=arecv.at[s],
            device_id={"dom": partner},
            device_id_type=MESH,
        )
        copy.start()
        started.append(copy)
        copy.wait_recv()
    gs_ref[...] = result[0:width, :]
    gn_ref[...] = result[width : 2 * width, :]
    for copy in started:
        copy.wait_send()

    def drain(j, carry):
        for k in range(nf - 1):
            partial_copy(k, j).wait_send()
            grad_copy(k, j).wait_send()
        return carry

    lax.fori_loop(0, chunks, drain, 0)


def layer(n, nf, features, aggregated, w_self, w_neigh, hidden_bias, cotangent):
    nodes, width = features.shape
    owned, units = cotangent.shape
    chunk = min(256, owned)
    chunks = owned // chunk
    plan = halving_plan(n, 2 * width)
    halves = []
    for _, halve, length in plan:
        one = [pltpu.VMEM((length, units), F32)]
        if not halve:
            one.append(pltpu.VMEM((length, units), F32))
        halves.append(tuple(one))
    steps = len(plan)
    dma = pltpu.SemaphoreType.DMA
    others = max(nf - 1, 1)
    return pl.pallas_call(
        functools.partial(layer_kernel, n, nf, plan, chunk),
        out_shape=(
            jax.ShapeDtypeStruct((owned, units), BF16),
            jax.ShapeDtypeStruct((width, units), BF16),
            jax.ShapeDtypeStruct((width, units), BF16),
            jax.ShapeDtypeStruct((8, units), F32),
        ),
        in_specs=[VMEM] * 6,
        out_specs=(VMEM,) * 4,
        scratch_shapes=[
            pltpu.VMEM((others, owned, units), F32),
            pltpu.VMEM((others, owned, units), F32),
            pltpu.VMEM((owned, units), F32),
            pltpu.VMEM((nodes, units), BF16),
            pltpu.VMEM((2 * width, units), F32),
            pltpu.VMEM((nf * chunks, 8, units), F32),
            pltpu.VMEM((2 * width, units), BF16),
            tuple(halves),
            pltpu.VMEM((2 * steps, 8, units), F32),
            dma((others, chunks)),
            dma((others, chunks)),
            dma((others, chunks)),
            dma((others, chunks)),
            dma((steps,)),
            dma((steps,)),
            dma((steps,)),
            dma((steps,)),
            dma((steps,)),
            dma((steps,)),
        ],
        compiler_params=pltpu.CompilerParams(
            collective_id=1, has_side_effects=True, vmem_limit_bytes=48 * 2**20
        ),
    )(features, aggregated, w_self, w_neigh, hidden_bias[None, :], cotangent)


def body(
    n, nf, features, w_self, w_neigh, hidden_bias, edge_tiles, tile_dst, tile_src, tile_count,
    bound_rows, send_pick, cotangent,
):
    received = received_blocks(n, features, bound_rows, send_pick[0])
    received = received.reshape(-1, features.shape[1])
    aggregated = aggregate(features, received, edge_tiles[0], tile_dst, tile_src, tile_count)
    hidden, grad_self, grad_neigh, grad_bias = layer(
        n, nf, features, aggregated, w_self, w_neigh, hidden_bias, cotangent
    )
    return hidden, grad_self, grad_neigh, grad_bias[0]


def solution(mesh):
    placed = (
        P("dom", "feat"),
        P("feat", None),
        P("feat", None),
        P(),
        P("dom", None, None, None),
        P("dom", None),
        P("dom", None),
        P("dom"),
        P("dom", None),
        P("dom", None, None),
        P(("dom", "feat"), None),
    )
    return jax.shard_map(
        functools.partial(body, mesh.shape["dom"], mesh.shape["feat"]),
        mesh=mesh,
        in_specs=placed,
        out_specs=(P(("dom", "feat"), None), P("feat", None), P("feat", None), P()),
        check_vma=False,
    )
```

```python
import functools

import jax
import jax.numpy as jnp
from jax import lax
from jax.experimental import pallas as pl
from jax.experimental.pallas import tpu as pltpu
from jax.sharding import PartitionSpec as P

LEVELS = 32767.0
TINY = 1e-30
MESH = pl.DeviceIdType.MESH
F32 = jnp.float32
BF16 = jnp.bfloat16
VMEM = pl.BlockSpec(memory_space=pltpu.VMEM)
SMEM = pl.BlockSpec(memory_space=pltpu.SMEM)
ANY = pl.BlockSpec(memory_space=pl.ANY)
TN = (((0,), (0,)), ((), ()))


def boundary_kernel(n, feat_ref, bound_ref, pick_ref, out_ref, blocks, send, recv, side_send, side_recv):
    chips = n // 2
    turn = chips // 2
    full = chips // 2 - 1
    ub = bound_ref.shape[1]
    width = feat_ref.shape[1]
    pick = pick_ref.shape[1]
    half_rows = ub // 2
    parts = ((0, half_rows), (half_rows, ub - half_rows + n))

    me = lax.axis_index("dom")
    core = me % 2
    chip = me // 2
    col = chip % 2
    row = chip // 2
    place = (1 - col) * row + col * (chips - 1 - row)

    def dom_of(position, which):
        position = (position + 2 * chips) % chips
        up = position // turn
        at = (1 - up) * 2 * position + up * (2 * (chips - 1 - position) + 1)
        return at * 2 + which

    ahead = dom_of(place + 1, core)
    behind = dom_of(place - 1, core)
    sibling = me + 1 - 2 * core

    barrier = pltpu.get_barrier_semaphore()
    for other in (ahead, behind, sibling):
        pl.semaphore_signal(barrier, inc=1, device_id={"dom": other}, device_id_type=MESH)

    nodes = feat_ref.shape[0]
    depth = min(512, nodes)
    wanted = bound_ref[0:1, :]

    def add_rows(k, total):
        ids = lax.broadcasted_iota(jnp.int32, (depth, ub), 0) + k * depth
        hot = jnp.where(ids == wanted, 1.0, 0.0).astype(BF16)
        rows = feat_ref[pl.ds(pl.multiple_of(k * depth, depth), depth), :]
        return total + lax.dot_general(hot, rows, TN, preferred_element_type=F32)

    total = lax.fori_loop(0, nodes // depth, add_rows, jnp.zeros((ub, width), F32))
    blocks[me, 0:ub, :] = total.astype(BF16)
    blocks[me, ub : ub + n, 0:pick] = pick_ref[...]
    if width > pick:
        blocks[me, ub : ub + n, pick:width] = jnp.zeros((n, width - pick), BF16)
    pl.semaphore_wait(barrier, 3)

    def hop(way, step, h):
        source = place - step if way == 0 else place + step
        owner = dom_of(source, core)
        at = blocks.at[owner, pl.ds(parts[h][0], parts[h][1])]
        return pltpu.make_async_remote_copy(
            src_ref=at,
            dst_ref=at,
            send_sem=send.at[way, step, h],
            recv_sem=recv.at[way, step, h],
            device_id={"dom": ahead if way == 0 else behind},
            device_id_type=MESH,
        )

    def aside(i, owner):
        return pltpu.make_async_remote_copy(
            src_ref=blocks.at[owner],
            dst_ref=blocks.at[owner],
            send_sem=side_send.at[i],
            recv_sem=side_recv.at[i],
            device_id={"dom": sibling},
            device_id_type=MESH,
        )

    def take(owner):
        table = blocks[owner, ub : ub + n, 0:pick].astype(F32)
        rows = lax.broadcasted_iota(jnp.int32, (n, pick), 0)
        mine = jnp.sum(jnp.where(rows == me, table, 0.0), axis=0, keepdims=True)
        ids = lax.broadcasted_iota(jnp.int32, (ub, pick), 0).astype(F32)
        hot = jnp.where(ids == mine, 1.0, 0.0).astype(BF16)
        got = lax.dot_general(hot, blocks[owner, 0:ub, :], TN, preferred_element_type=F32)
        out_ref[owner] = got.astype(BF16)

    started = []
    sides = []
    side_seen = 0

    def arrived(position):
        i = len(sides)
        copy = aside(i, dom_of(position, core))
        copy.start()
        sides.append((copy, position))

    for step in range(full + 1):
        for h in (0, 1):
            for way in (0, 1):
                if step > 0:
                    hop(way, step - 1, h).wait_recv()
                if step < full or h == way:
                    copy = hop(way, step, h)
                    copy.start()
                    started.append(copy)
        if step == 0:
            arrived(place)
            take(me)
        else:
            for position in (place - step, place + step):
                arrived(position)
                take(dom_of(position, core))
            while side_seen < len(sides) - 2:
                copy, position = sides[side_seen]
                copy.wait_recv()
                take(dom_of(position, 1 - core))
                side_seen += 1
    hop(0, full, 0).wait_recv()
    hop(1, full, 1).wait_recv()
    arrived(place + full + 1)
    take(dom_of(place + full + 1, core))
    while side_seen < len(sides):
        copy, position = sides[side_seen]
        copy.wait_recv()
        take(dom_of(position, 1 - core))
        side_seen += 1
    for copy in started:
        copy.wait_send()
    for copy, _ in sides:
        copy.wait_send()


def received_blocks(n, features, bound_rows, send_pick):
    width = features.shape[1]
    ub = bound_rows.shape[1]
    pick = send_pick.shape[1]
    steps = n // 4
    return pl.pallas_call(
        functools.partial(boundary_kernel, n),
        out_shape=jax.ShapeDtypeStruct((n, pick, width), BF16),
        in_specs=[VMEM] * 3,
        out_specs=VMEM,
        scratch_shapes=[
            pltpu.VMEM((n, ub + n, width), BF16),
            pltpu.SemaphoreType.DMA((2, steps, 2)),
            pltpu.SemaphoreType.DMA((2, steps, 2)),
            pltpu.SemaphoreType.DMA((n // 2,)),
            pltpu.SemaphoreType.DMA((n // 2,)),
        ],
        compiler_params=pltpu.CompilerParams(
            collective_id=0, has_side_effects=True, vmem_limit_bytes=40 * 2**20
        ),
    )(features, bound_rows, send_pick.astype(BF16))


def tile_kernel(group, dst_ref, src_ref, count_ref, feat_ref, recv_ref, tiles_ref, out_ref, source, total, sems):
    tile = tiles_ref.shape[1]
    nodes = feat_ref.shape[0]
    copies = (
        pltpu.make_async_copy(feat_ref, source.at[pl.ds(0, nodes)], sems.at[0]),
        pltpu.make_async_copy(recv_ref, source.at[pl.ds(nodes, recv_ref.shape[0])], sems.at[1]),
    )
    for copy in copies:
        copy.start()
    total[...] = jnp.zeros_like(total)
    for copy in copies:
        copy.wait()
    count = count_ref[0]

    def slots(g, carry):
        products = []
        for u in range(group):
            e = g * group + u
            block = source[pl.ds(pl.multiple_of(src_ref[0, e] * tile, tile), tile), :]
            product = jnp.dot(tiles_ref[e], block, preferred_element_type=F32)
            products.append(jnp.where(e < count, product, 0.0))
        for u in range(group):
            e = g * group + u
            at = pl.ds(pl.multiple_of(dst_ref[0, e] * tile, tile), tile)
            total[at, :] += products[u]
        return carry

    lax.fori_loop(0, (count + group - 1) // group, slots, 0)
    out_ref[...] = total[...].astype(BF16)


def aggregate(features, received, edge_tiles, tile_dst, tile_src, tile_count):
    nodes, width = features.shape
    slots = edge_tiles.shape[0]
    group = next(g for g in (3, 2, 1) if slots % g == 0)
    rows = received.shape[0]
    return pl.pallas_call(
        functools.partial(tile_kernel, group),
        out_shape=jax.ShapeDtypeStruct((nodes, width), BF16),
        in_specs=[SMEM, SMEM, SMEM, ANY, ANY, VMEM],
        out_specs=VMEM,
        scratch_shapes=[
            pltpu.VMEM((nodes + rows, width), BF16),
            pltpu.VMEM((nodes, width), F32),
            pltpu.SemaphoreType.DMA((2,)),
        ],
        compiler_params=pltpu.CompilerParams(vmem_limit_bytes=40 * 2**20),
    )(tile_dst, tile_src, tile_count, features, received, edge_tiles)


def halving_plan(n, rows):
    plan = []
    length = rows
    bit = 1
    while bit < n:
        halve = length % 32 == 0
        if halve:
            length //= 2
        plan.append((bit, halve, length))
        bit *= 2
    return plan


def layer_kernel(
    n, nf, plan, chunk,
    feat_ref, agg_ref, ws_ref, wn_ref, bias_ref, cot_ref,
    hidden_ref, gs_ref, gn_ref, gb_ref,
    outgoing, incoming, scales, own, grads, total, sums, result, halves, small,
    psend, precv, ssend, srecv, gsend, grecv, hsend, hrecv, bsend, brecv, asend, arecv,
):
    me = lax.axis_index("dom")
    f = lax.axis_index("feat")
    owned = cot_ref.shape[0]
    width = feat_ref.shape[1]
    chunks = owned // chunk
    partners = []
    for bit, _, _ in plan:
        side = (me // bit) % 2
        partners.append((me + bit - 2 * bit * side, side))
    peers = [(f + k) % nf for k in range(1, nf)]

    barrier = pltpu.get_barrier_semaphore()
    for peer in peers:
        pl.semaphore_signal(barrier, inc=1, device_id={"feat": peer}, device_id_type=MESH)
    for partner, _ in partners:
        pl.semaphore_signal(barrier, inc=1, device_id={"dom": partner}, device_id_type=MESH)
    pl.semaphore_wait(barrier, nf - 1 + len(plan))

    def at_rows(owner, j):
        return pl.ds(pl.multiple_of(owner * owned + j * chunk, chunk), chunk)

    def partial(owner, j):
        rows = at_rows(owner, j)
        return jnp.dot(feat_ref[rows, :], ws_ref[...], preferred_element_type=F32) + jnp.dot(
            agg_ref[rows, :], wn_ref[...], preferred_element_type=F32
        )

    def inside(j):
        return pl.ds(pl.multiple_of(j * chunk, chunk), chunk)

    def partial_copy(k, j):
        return pltpu.make_async_remote_copy(
            src_ref=outgoing.at[k, inside(j)],
            dst_ref=incoming.at[k, inside(j)],
            send_sem=psend.at[k, j],
            recv_sem=precv.at[k, j],
            device_id={"feat": peers[k]},
            device_id_type=MESH,
        )

    def scale_copy(k, j):
        return pltpu.make_async_remote_copy(
            src_ref=scales.at[0, k, j],
            dst_ref=scales.at[1, k, j],
            send_sem=ssend.at[k, j],
            recv_sem=srecv.at[k, j],
            device_id={"feat": peers[k]},
            device_id_type=MESH,
        )

    units = cot_ref.shape[1]
    span = chunk // 8

    def grad_copy(k, j):
        rows = at_rows(f, j)
        return pltpu.make_async_remote_copy(
            src_ref=grads.at[rows],
            dst_ref=grads.at[rows],
            send_sem=gsend.at[k, j],
            recv_sem=grecv.at[k, j],
            device_id={"feat": peers[k]},
            device_id_type=MESH,
        )

    def send_partials(j, carry):
        for k in range(nf - 1):
            value = partial(peers[k], j).reshape(8, span, units)
            top = jnp.max(jnp.max(jnp.abs(value), axis=1), axis=1, keepdims=True)
            top = jnp.broadcast_to(jnp.maximum(top, TINY), (8, units))
            scales[0, k, j] = top * (1.0 / LEVELS)
            steps = jnp.round(value * (LEVELS / top)[:, None, :])
            steps = steps.reshape(chunk, units).astype(jnp.int32)
            outgoing[k, inside(j), :] = steps.astype(jnp.int16)
            scale_copy(k, j).start()
            partial_copy(k, j).start()
        return carry

    lax.fori_loop(0, chunks, send_partials, 0)

    def own_partials(j, carry):
        own[inside(j), :] = partial(f, j)
        return carry

    lax.fori_loop(0, chunks, own_partials, 0)
    total[...] = jnp.zeros_like(total)

    def add_grads(owner, j):
        rows = at_rows(owner, j)
        block = grads[rows, :]
        total[0:width, :] += lax.dot_general(feat_ref[rows, :], block, TN, preferred_element_type=F32)
        total[width : 2 * width, :] += lax.dot_general(
            agg_ref[rows, :], block, TN, preferred_element_type=F32
        )
        wide = block.astype(F32).reshape(chunk // 8, 8, block.shape[1])
        sums[owner * chunks + j] = jnp.sum(wide, axis=0)

    def finish_rows(j, carry):
        for k in range(nf - 1):
            scale_copy(k, j).wait_recv()
            partial_copy(k, j).wait_recv()
        preact = own[inside(j), :]
        for k in range(nf - 1):
            steps = incoming[k, inside(j), :].astype(jnp.int32).astype(F32)
            value = steps.reshape(8, span, units) * scales[1, k, j][:, None, :]
            preact = preact + value.reshape(chunk, units)
        preact = preact + bias_ref[...]
        hidden_ref[inside(j), :] = jnp.maximum(preact, 0.0).astype(BF16)
        grads[at_rows(f, j), :] = jnp.where(preact > 0.0, cot_ref[inside(j), :].astype(F32), 0.0).astype(BF16)
        for k in range(nf - 1):
            grad_copy(k, j).start()
        add_grads(f, j)
        return carry

    lax.fori_loop(0, chunks, finish_rows, 0)

    def other_rows(j, carry):
        for k in range(nf - 1):
            owner = (f + nf - 1 - k) % nf
            grad_copy(k, j).wait_recv()
            add_grads(owner, j)
        return carry

    lax.fori_loop(0, chunks, other_rows, 0)

    def add_sums(i, acc):
        return acc + sums[i]

    bias_sum = lax.fori_loop(0, nf * chunks, add_sums, jnp.zeros(sums.shape[1:], F32))
    bias_sum = jnp.broadcast_to(jnp.sum(bias_sum, axis=0, keepdims=True), bias_sum.shape)

    started = []
    base = 0
    bases = []
    for s, (bit, halve, length) in enumerate(plan):
        partner, side = partners[s]
        bases.append(base)
        if halve:
            keep = base + side * length
            give = base + (1 - side) * length
        else:
            keep = give = base
        keep_rows = pl.ds(pl.multiple_of(keep, 16), length)
        give_rows = pl.ds(pl.multiple_of(give, 16), length)
        small[2 * s] = bias_sum
        copy = pltpu.make_async_remote_copy(
            src_ref=halves[s][1] if len(halves[s]) > 1 else total.at[give_rows],
            dst_ref=halves[s][0],
            send_sem=hsend.at[s],
            recv_sem=hrecv.at[s],
            device_id={"dom": partner},
            device_id_type=MESH,
        )
        if len(halves[s]) > 1:
            halves[s][1][...] = total[give_rows, :].astype(halves[s][1].dtype)
        copy.start()
        tiny = pltpu.make_async_remote_copy(
            src_ref=small.at[2 * s],
            dst_ref=small.at[2 * s + 1],
            send_sem=bsend.at[s],
            recv_sem=brecv.at[s],
            device_id={"dom": partner},
            device_id_type=MESH,
        )
        tiny.start()
        started += [copy, tiny]
        copy.wait_recv()
        total[keep_rows, :] += halves[s][0][...].astype(F32)
        tiny.wait_recv()
        bias_sum = bias_sum + small[2 * s + 1]
        base = keep
    last = plan[-1][2]
    rows = pl.ds(pl.multiple_of(base, 16), last)
    result[rows, :] = total[rows, :].astype(BF16)
    gb_ref[...] = bias_sum
    held = last
    for s in range(len(plan) - 1, -1, -1):
        bit, halve, length = plan[s]
        if not halve:
            continue
        partner, side = partners[s]
        mine = pl.ds(pl.multiple_of(bases[s] + side * length, 16), length)
        copy = pltpu.make_async_remote_copy(
            src_ref=result.at[mine],
            dst_ref=result.at[mine],
            send_sem=asend.at[s],
            recv_sem=arecv.at[s],
            device_id={"dom": partner},
            device_id_type=MESH,
        )
        copy.start()
        started.append(copy)
        copy.wait_recv()
    gs_ref[...] = result[0:width, :]
    gn_ref[...] = result[width : 2 * width, :]
    for copy in started:
        copy.wait_send()

    def drain(j, carry):
        for k in range(nf - 1):
            scale_copy(k, j).wait_send()
            partial_copy(k, j).wait_send()
            grad_copy(k, j).wait_send()
        return carry

    lax.fori_loop(0, chunks, drain, 0)


def layer(n, nf, features, aggregated, w_self, w_neigh, hidden_bias, cotangent):
    nodes, width = features.shape
    owned, units = cotangent.shape
    chunk = min(256, owned)
    chunks = owned // chunk
    plan = halving_plan(n, 2 * width)
    halves = []
    for bit, halve, length in plan:
        kind = BF16 if halve and bit > 1 else F32
        one = [pltpu.VMEM((length, units), kind)]
        if kind == BF16 or not halve:
            one.append(pltpu.VMEM((length, units), kind))
        halves.append(tuple(one))
    steps = len(plan)
    dma = pltpu.SemaphoreType.DMA
    others = max(nf - 1, 1)
    return pl.pallas_call(
        functools.partial(layer_kernel, n, nf, plan, chunk),
        out_shape=(
            jax.ShapeDtypeStruct((owned, units), BF16),
            jax.ShapeDtypeStruct((width, units), BF16),
            jax.ShapeDtypeStruct((width, units), BF16),
            jax.ShapeDtypeStruct((8, units), F32),
        ),
        in_specs=[VMEM] * 6,
        out_specs=(VMEM,) * 4,
        scratch_shapes=[
            pltpu.VMEM((others, owned, units), jnp.int16),
            pltpu.VMEM((others, owned, units), jnp.int16),
            pltpu.VMEM((2, others, chunks, 8, units), F32),
            pltpu.VMEM((owned, units), F32),
            pltpu.VMEM((nodes, units), BF16),
            pltpu.VMEM((2 * width, units), F32),
            pltpu.VMEM((nf * chunks, 8, units), F32),
            pltpu.VMEM((2 * width, units), BF16),
            tuple(halves),
            pltpu.VMEM((2 * steps, 8, units), F32),
            dma((others, chunks)),
            dma((others, chunks)),
            dma((others, chunks)),
            dma((others, chunks)),
            dma((others, chunks)),
            dma((others, chunks)),
            dma((steps,)),
            dma((steps,)),
            dma((steps,)),
            dma((steps,)),
            dma((steps,)),
            dma((steps,)),
        ],
        compiler_params=pltpu.CompilerParams(
            collective_id=1, has_side_effects=True, vmem_limit_bytes=28 * 2**20
        ),
    )(features, aggregated, w_self, w_neigh, hidden_bias[None, :], cotangent)


def body(
    n, nf, features, w_self, w_neigh, hidden_bias, edge_tiles, tile_dst, tile_src, tile_count,
    bound_rows, send_pick, cotangent,
):
    received = received_blocks(n, features, bound_rows, send_pick[0])
    received = received.reshape(-1, features.shape[1])
    aggregated = aggregate(features, received, edge_tiles[0], tile_dst, tile_src, tile_count)
    hidden, grad_self, grad_neigh, grad_bias = layer(
        n, nf, features, aggregated, w_self, w_neigh, hidden_bias, cotangent
    )
    return hidden, grad_self, grad_neigh, grad_bias[0]


def solution(mesh):
    placed = (
        P("dom", "feat"),
        P("feat", None),
        P("feat", None),
        P(),
        P("dom", None, None, None),
        P("dom", None),
        P("dom", None),
        P("dom"),
        P("dom", None),
        P("dom", None, None),
        P(("dom", "feat"), None),
    )
    return jax.shard_map(
        functools.partial(body, mesh.shape["dom"], mesh.shape["feat"]),
        mesh=mesh,
        in_specs=placed,
        out_specs=(P(("dom", "feat"), None), P("feat", None), P("feat", None), P()),
        check_vma=False,
    )
```

```python
import functools

import jax
import jax.numpy as jnp
from jax import lax
from jax.experimental import pallas as pl
from jax.experimental.pallas import tpu as pltpu
from jax.sharding import PartitionSpec as P

LEVELS = 32767.0
TINY = 1e-30
AHEAD = 4
LAG = 3
MESH = pl.DeviceIdType.MESH
F32 = jnp.float32
BF16 = jnp.bfloat16
VMEM = pl.BlockSpec(memory_space=pltpu.VMEM)
SMEM = pl.BlockSpec(memory_space=pltpu.SMEM)
TN = (((0,), (0,)), ((), ()))


def boundary_kernel(n, feat_ref, bound_ref, pick_ref, out_ref, blocks, send, recv, side_send, side_recv, local):
    chips = n // 2
    turn = chips // 2
    full = chips // 2 - 1
    ub = bound_ref.shape[1]
    width = feat_ref.shape[1]
    pick = pick_ref.shape[1]
    half_rows = ub // 2
    parts = ((0, half_rows), (half_rows, ub - half_rows + n))

    me = lax.axis_index("dom")
    core = me % 2
    chip = me // 2
    col = chip % 2
    row = chip // 2
    place = (1 - col) * row + col * (chips - 1 - row)

    def dom_of(position, which):
        position = (position + 2 * chips) % chips
        up = position // turn
        at = (1 - up) * 2 * position + up * (2 * (chips - 1 - position) + 1)
        return at * 2 + which

    ahead = dom_of(place + 1, core)
    behind = dom_of(place - 1, core)
    sibling = me + 1 - 2 * core

    barrier = pltpu.get_barrier_semaphore()
    for other in (ahead, behind, sibling):
        pl.semaphore_signal(barrier, inc=1, device_id={"dom": other}, device_id_type=MESH)

    nodes = feat_ref.shape[0]
    kept = pltpu.make_async_copy(feat_ref, out_ref.at[pl.ds(0, nodes)], local.at[0])
    kept.start()
    depth = min(512, nodes)
    wanted = bound_ref[0:1, :]

    def add_rows(k, total):
        ids = lax.broadcasted_iota(jnp.int32, (depth, ub), 0) + k * depth
        hot = jnp.where(ids == wanted, 1.0, 0.0).astype(BF16)
        rows = feat_ref[pl.ds(pl.multiple_of(k * depth, depth), depth), :]
        return total + lax.dot_general(hot, rows, TN, preferred_element_type=F32)

    total = lax.fori_loop(0, nodes // depth, add_rows, jnp.zeros((ub, width), F32))
    blocks[me, 0:ub, :] = total.astype(BF16)
    blocks[me, ub : ub + n, 0:pick] = pick_ref[...]
    if width > pick:
        blocks[me, ub : ub + n, pick:width] = jnp.zeros((n, width - pick), BF16)
    pl.semaphore_wait(barrier, 3)

    def hop(way, step, h):
        source = place - step if way == 0 else place + step
        owner = dom_of(source, core)
        at = blocks.at[owner, pl.ds(parts[h][0], parts[h][1])]
        return pltpu.make_async_remote_copy(
            src_ref=at,
            dst_ref=at,
            send_sem=send.at[way, step, h],
            recv_sem=recv.at[way, step, h],
            device_id={"dom": ahead if way == 0 else behind},
            device_id_type=MESH,
        )

    def aside(i, owner):
        return pltpu.make_async_remote_copy(
            src_ref=blocks.at[owner],
            dst_ref=blocks.at[owner],
            send_sem=side_send.at[i],
            recv_sem=side_recv.at[i],
            device_id={"dom": sibling},
            device_id_type=MESH,
        )

    def take(owner):
        table = blocks[owner, ub : ub + n, 0:pick].astype(F32)
        rows = lax.broadcasted_iota(jnp.int32, (n, pick), 0)
        mine = jnp.sum(jnp.where(rows == me, table, 0.0), axis=0, keepdims=True)
        ids = lax.broadcasted_iota(jnp.int32, (ub, pick), 0).astype(F32)
        hot = jnp.where(ids == mine, 1.0, 0.0).astype(BF16)
        got = lax.dot_general(hot, blocks[owner, 0:ub, :], TN, preferred_element_type=F32)
        at = pl.ds(pl.multiple_of(nodes + owner * pick, pick), pick)
        out_ref[at, :] = got.astype(BF16)

    started = []
    sides = []
    side_seen = 0

    def arrived(position):
        i = len(sides)
        copy = aside(i, dom_of(position, core))
        copy.start()
        sides.append((copy, position))

    for step in range(full + 1):
        for h in (0, 1):
            for way in (0, 1):
                if step > 0:
                    hop(way, step - 1, h).wait_recv()
                if step < full or h == way:
                    copy = hop(way, step, h)
                    copy.start()
                    started.append(copy)
        if step == 0:
            arrived(place)
            take(me)
        else:
            for position in (place - step, place + step):
                arrived(position)
                take(dom_of(position, core))
            while side_seen < len(sides) - 2:
                copy, position = sides[side_seen]
                copy.wait_recv()
                take(dom_of(position, 1 - core))
                side_seen += 1
    hop(0, full, 0).wait_recv()
    hop(1, full, 1).wait_recv()
    arrived(place + full + 1)
    take(dom_of(place + full + 1, core))
    while side_seen < len(sides):
        copy, position = sides[side_seen]
        copy.wait_recv()
        take(dom_of(position, 1 - core))
        side_seen += 1
    for copy in started:
        copy.wait_send()
    for copy, _ in sides:
        copy.wait_send()
    kept.wait()


def source_rows(n, features, bound_rows, send_pick):
    width = features.shape[1]
    ub = bound_rows.shape[1]
    pick = send_pick.shape[1]
    steps = n // 4
    return pl.pallas_call(
        functools.partial(boundary_kernel, n),
        out_shape=jax.ShapeDtypeStruct((features.shape[0] + n * pick, width), BF16),
        in_specs=[VMEM] * 3,
        out_specs=VMEM,
        scratch_shapes=[
            pltpu.VMEM((n, ub + n, width), BF16),
            pltpu.SemaphoreType.DMA((2, steps, 2)),
            pltpu.SemaphoreType.DMA((2, steps, 2)),
            pltpu.SemaphoreType.DMA((n // 2,)),
            pltpu.SemaphoreType.DMA((n // 2,)),
            pltpu.SemaphoreType.DMA((1,)),
        ],
        compiler_params=pltpu.CompilerParams(
            collective_id=0, has_side_effects=True, vmem_limit_bytes=40 * 2**20
        ),
    )(features, bound_rows, send_pick.astype(BF16))


def tile_kernel(group, dst_ref, src_ref, count_ref, source_ref, tiles_ref, out_ref, total):
    tile = tiles_ref.shape[1]
    total[...] = jnp.zeros_like(total)
    count = count_ref[0]

    def slots(g, carry):
        products = []
        for u in range(group):
            e = g * group + u
            block = source_ref[pl.ds(pl.multiple_of(src_ref[0, e] * tile, tile), tile), :]
            product = jnp.dot(tiles_ref[e], block, preferred_element_type=F32)
            products.append(jnp.where(e < count, product, 0.0))
        for u in range(group):
            e = g * group + u
            at = pl.ds(pl.multiple_of(dst_ref[0, e] * tile, tile), tile)
            total[at, :] += products[u]
        return carry

    lax.fori_loop(0, (count + group - 1) // group, slots, 0)
    out_ref[...] = total[...].astype(BF16)


def aggregate(nodes, source, edge_tiles, tile_dst, tile_src, tile_count):
    width = source.shape[1]
    slots = edge_tiles.shape[0]
    group = next(g for g in (3, 2, 1) if slots % g == 0)
    return pl.pallas_call(
        functools.partial(tile_kernel, group),
        out_shape=jax.ShapeDtypeStruct((nodes, width), BF16),
        in_specs=[SMEM, SMEM, SMEM, VMEM, VMEM],
        out_specs=VMEM,
        scratch_shapes=[pltpu.VMEM((nodes, width), F32)],
        compiler_params=pltpu.CompilerParams(vmem_limit_bytes=30 * 2**20),
    )(tile_dst, tile_src, tile_count, source, edge_tiles)


def halving_plan(n, rows):
    plan = []
    length = rows
    bit = 1
    while bit < n:
        halve = length % 32 == 0
        if halve:
            length //= 2
        plan.append((bit, halve, length))
        bit *= 2
    return plan


def layer_kernel(
    n, nf, plan, chunk, waves,
    feat_ref, agg_ref, ws_ref, wn_ref, bias_ref, cot_ref,
    hidden_ref, gs_ref, gn_ref, gb_ref,
    outgoing, incoming, scales, grads, total, sums, result, halves, small,
    psend, precv, ssend, srecv, gsend, grecv, hsend, hrecv, bsend, brecv, asend, arecv,
):
    me = lax.axis_index("dom")
    f = lax.axis_index("feat")
    owned, units = cot_ref.shape
    width = feat_ref.shape[1]
    chunks = owned // chunk
    lanes = units // waves
    items = waves * chunks
    ahead = min(AHEAD, items)
    lag = min(LAG, chunks)
    span = chunk // 8
    partners = []
    for bit, _, _ in plan:
        side = (me // bit) % 2
        partners.append((me + bit - 2 * bit * side, side))
    peers = [(f + k) % nf for k in range(1, nf)]

    barrier = pltpu.get_barrier_semaphore()
    for peer in peers:
        pl.semaphore_signal(barrier, inc=1, device_id={"feat": peer}, device_id_type=MESH)
    for partner, _ in partners:
        pl.semaphore_signal(barrier, inc=1, device_id={"dom": partner}, device_id_type=MESH)
    total[...] = jnp.zeros_like(total)
    pl.semaphore_wait(barrier, nf - 1 + len(plan))

    def at_rows(owner, j):
        return pl.ds(pl.multiple_of(owner * owned + j * chunk, chunk), chunk)

    def at_units(w):
        return pl.ds(pl.multiple_of(w * lanes, lanes), lanes)

    def inside(j):
        return pl.ds(pl.multiple_of(j * chunk, chunk), chunk)

    def partial(owner, j, w):
        rows = at_rows(owner, j)
        cols = at_units(w)
        return jnp.dot(feat_ref[rows, :], ws_ref[:, cols], preferred_element_type=F32) + jnp.dot(
            agg_ref[rows, :], wn_ref[:, cols], preferred_element_type=F32
        )

    def push(src, dst, send_sem, recv_sem, axis, to):
        return pltpu.make_async_remote_copy(
            src_ref=src,
            dst_ref=dst,
            send_sem=send_sem,
            recv_sem=recv_sem,
            device_id={axis: to},
            device_id_type=MESH,
        )

    def partial_copy(k, i):
        return push(
            outgoing.at[k, i], incoming.at[k, i], psend.at[k, i], precv.at[k, i], "feat", peers[k]
        )

    def scale_copy(k, i):
        return push(
            scales.at[0, k, i], scales.at[1, k, i], ssend.at[k, i], srecv.at[k, i], "feat", peers[k]
        )

    def grad_copy(k, i):
        at = grads.at[i // chunks, at_rows(f, i % chunks)]
        return push(at, at, gsend.at[k, i], grecv.at[k, i], "feat", peers[k])

    def send_partial(i):
        w, j = i // chunks, i % chunks
        for k in range(nf - 1):
            value = partial(peers[k], j, w).reshape(8, span, lanes)
            top = jnp.max(jnp.max(jnp.abs(value), axis=1), axis=1, keepdims=True)
            top = jnp.broadcast_to(jnp.maximum(top, TINY), (8, lanes))
            scales[0, k, i] = top * (1.0 / LEVELS)
            steps = jnp.round(value * (LEVELS / top)[:, None, :])
            steps = steps.reshape(chunk, lanes).astype(jnp.int32)
            outgoing[k, i] = steps.astype(jnp.int16)
            scale_copy(k, i).start()
            partial_copy(k, i).start()

    def add_grads(owner, i):
        w, j = i // chunks, i % chunks
        rows = at_rows(owner, j)
        block = grads[w, rows, :]
        total[w, 0:width, :] += lax.dot_general(
            feat_ref[rows, :], block, TN, preferred_element_type=F32
        )
        total[w, width : 2 * width, :] += lax.dot_general(
            agg_ref[rows, :], block, TN, preferred_element_type=F32
        )
        wide = block.astype(F32).reshape(chunk // 8, 8, lanes)
        sums[w, owner * chunks + j] = jnp.sum(wide, axis=0)

    def finish(i):
        w, j = i // chunks, i % chunks
        preact = partial(f, j, w)
        cols = at_units(w)
        for k in range(nf - 1):
            scale_copy(k, i).wait_recv()
            partial_copy(k, i).wait_recv()
        for k in range(nf - 1):
            steps = incoming[k, i].astype(jnp.int32).astype(F32)
            value = steps.reshape(8, span, lanes) * scales[1, k, i][:, None, :]
            preact = preact + value.reshape(chunk, lanes)
        preact = preact + bias_ref[:, cols]
        kept = jnp.where(preact > 0.0, cot_ref[inside(j), cols].astype(F32), 0.0)
        grads[w, at_rows(f, j), :] = kept.astype(BF16)
        for k in range(nf - 1):
            grad_copy(k, i).start()
        hidden_ref[inside(j), cols] = jnp.maximum(preact, 0.0).astype(BF16)

    def others(i):
        for k in range(nf - 1):
            grad_copy(k, i).wait_recv()
            add_grads((f + nf - 1 - k) % nf, i)

    def each(low, high, do):
        def step(i, carry):
            do(i)
            return carry

        if high > low:
            lax.fori_loop(low, high, step, 0)

    started = []

    def reduction(w):
        bias_sum = lax.fori_loop(
            0, nf * chunks, lambda i, acc: acc + sums[w, i], jnp.zeros(sums.shape[2:], F32)
        )
        bias_sum = jnp.broadcast_to(jnp.sum(bias_sum, axis=0, keepdims=True), bias_sum.shape)
        base = 0
        bases = []
        for s, (bit, halve, length) in enumerate(plan):
            partner, side = partners[s]
            bases.append(base)
            if halve:
                keep = base + side * length
                give = base + (1 - side) * length
            else:
                keep = give = base
            keep_rows = pl.ds(pl.multiple_of(keep, 16), length)
            give_rows = pl.ds(pl.multiple_of(give, 16), length)
            small[w, 2 * s] = bias_sum
            staged = len(halves[s]) > 1
            if staged:
                halves[s][1][w] = total[w, give_rows, :].astype(halves[s][1].dtype)
            copy = push(
                halves[s][1].at[w] if staged else total.at[w, give_rows],
                halves[s][0].at[w],
                hsend.at[w, s],
                hrecv.at[w, s],
                "dom",
                partner,
            )
            copy.start()
            tiny = push(
                small.at[w, 2 * s], small.at[w, 2 * s + 1], bsend.at[w, s], brecv.at[w, s], "dom", partner
            )
            tiny.start()
            started.extend((copy, tiny))
            yield
            copy.wait_recv()
            total[w, keep_rows, :] += halves[s][0][w].astype(F32)
            tiny.wait_recv()
            bias_sum = bias_sum + small[w, 2 * s + 1]
            base = keep
        last = plan[-1][2]
        rows = pl.ds(pl.multiple_of(base, 16), last)
        result[w, rows, :] = total[w, rows, :].astype(BF16)
        gb_ref[:, w * lanes : (w + 1) * lanes] = bias_sum
        for s in range(len(plan) - 1, -1, -1):
            bit, halve, length = plan[s]
            if not halve:
                continue
            partner, side = partners[s]
            at = result.at[w, pl.ds(pl.multiple_of(bases[s] + side * length, 16), length)]
            copy = push(at, at, asend.at[w, s], arecv.at[w, s], "dom", partner)
            copy.start()
            started.append(copy)
            yield
            copy.wait_recv()
        gs_ref[:, w * lanes : (w + 1) * lanes] = result[w, 0:width, :]
        gn_ref[:, w * lanes : (w + 1) * lanes] = result[w, width : 2 * width, :]

    def item(i):
        finish(i)

        @pl.when(i + ahead < items)
        def _():
            send_partial(i + ahead)

        add_grads(f, i)

        @pl.when(i >= lag)
        def _():
            others(i - lag)

    each(0, ahead, send_partial)
    running = [reduction(w) for w in range(waves - 1)]
    first = (waves - 1) * chunks + lag if waves > 1 else items
    each(0, first, item)
    for i in range(first, items):
        running = [r for r in running if next(r, 0) is None]
        item(i)
    for i in range(items - lag, items):
        others(i)
        running = [r for r in running if next(r, 0) is None]
    running = [reduction(waves - 1)] + running
    while running:
        running = [r for r in running if next(r, 0) is None]
    for copy in started:
        copy.wait_send()

    def drain(i):
        for k in range(nf - 1):
            scale_copy(k, i).wait_send()
            partial_copy(k, i).wait_send()
            grad_copy(k, i).wait_send()

    each(0, items, drain)


def layer(n, nf, features, aggregated, w_self, w_neigh, hidden_bias, cotangent):
    nodes, width = features.shape
    owned, units = cotangent.shape
    chunk = min(256, owned)
    chunks = owned // chunk
    waves = 2 if units % 256 == 0 else 1
    lanes = units // waves
    items = waves * chunks
    plan = halving_plan(n, 2 * width)
    halves = []
    for bit, halve, length in plan:
        kind = BF16 if halve and bit > 1 else F32
        one = [pltpu.VMEM((waves, length, lanes), kind)]
        if kind == BF16 or not halve:
            one.append(pltpu.VMEM((waves, length, lanes), kind))
        halves.append(tuple(one))
    steps = len(plan)
    dma = pltpu.SemaphoreType.DMA
    others = max(nf - 1, 1)
    return pl.pallas_call(
        functools.partial(layer_kernel, n, nf, plan, chunk, waves),
        out_shape=(
            jax.ShapeDtypeStruct((owned, units), BF16),
            jax.ShapeDtypeStruct((width, units), BF16),
            jax.ShapeDtypeStruct((width, units), BF16),
            jax.ShapeDtypeStruct((8, units), F32),
        ),
        in_specs=[VMEM] * 6,
        out_specs=(VMEM,) * 4,
        scratch_shapes=[
            pltpu.VMEM((others, items, chunk, lanes), jnp.int16),
            pltpu.VMEM((others, items, chunk, lanes), jnp.int16),
            pltpu.VMEM((2, others, items, 8, lanes), F32),
            pltpu.VMEM((waves, nodes, lanes), BF16),
            pltpu.VMEM((waves, 2 * width, lanes), F32),
            pltpu.VMEM((waves, nf * chunks, 8, lanes), F32),
            pltpu.VMEM((waves, 2 * width, lanes), BF16),
            tuple(halves),
            pltpu.VMEM((waves, 2 * steps, 8, lanes), F32),
        ]
        + [dma((others, items))] * 6
        + [dma((waves, steps))] * 6,
        compiler_params=pltpu.CompilerParams(
            collective_id=1, has_side_effects=True, vmem_limit_bytes=28 * 2**20
        ),
    )(features, aggregated, w_self, w_neigh, hidden_bias[None, :], cotangent)


def body(
    n, nf, features, w_self, w_neigh, hidden_bias, edge_tiles, tile_dst, tile_src, tile_count,
    bound_rows, send_pick, cotangent,
):
    source = source_rows(n, features, bound_rows, send_pick[0])
    aggregated = aggregate(
        features.shape[0], source, edge_tiles[0], tile_dst, tile_src, tile_count
    )
    hidden, grad_self, grad_neigh, grad_bias = layer(
        n, nf, features, aggregated, w_self, w_neigh, hidden_bias, cotangent
    )
    return hidden, grad_self, grad_neigh, grad_bias[0]


def solution(mesh):
    placed = (
        P("dom", "feat"),
        P("feat", None),
        P("feat", None),
        P(),
        P("dom", None, None, None),
        P("dom", None),
        P("dom", None),
        P("dom"),
        P("dom", None),
        P("dom", None, None),
        P(("dom", "feat"), None),
    )
    return jax.shard_map(
        functools.partial(body, mesh.shape["dom"], mesh.shape["feat"]),
        mesh=mesh,
        in_specs=placed,
        out_specs=(P(("dom", "feat"), None), P("feat", None), P("feat", None), P()),
        check_vma=False,
    )
```

```python
import functools

import jax
import jax.numpy as jnp
from jax import lax
from jax.experimental import pallas as pl
from jax.experimental.pallas import tpu as pltpu
from jax.sharding import PartitionSpec as P

LEVELS = 32767.0
TINY = 1e-30
AHEAD = 4
LAG = 3
MESH = pl.DeviceIdType.MESH
F32 = jnp.float32
BF16 = jnp.bfloat16
VMEM = pl.BlockSpec(memory_space=pltpu.VMEM)
SMEM = pl.BlockSpec(memory_space=pltpu.SMEM)
TN = (((0,), (0,)), ((), ()))


def boundary_kernel(n, feat_ref, bound_ref, pick_ref, out_ref, blocks, send, recv, side_send, side_recv, local):
    chips = n // 2
    turn = chips // 2
    full = chips // 2 - 1
    ub = bound_ref.shape[1]
    width = feat_ref.shape[1]
    pick = pick_ref.shape[1]
    half_rows = ub // 2
    parts = ((0, half_rows), (half_rows, ub - half_rows + n))

    me = lax.axis_index("dom")
    core = me % 2
    chip = me // 2
    col = chip % 2
    row = chip // 2
    place = (1 - col) * row + col * (chips - 1 - row)

    def dom_of(position, which):
        position = (position + 2 * chips) % chips
        up = position // turn
        at = (1 - up) * 2 * position + up * (2 * (chips - 1 - position) + 1)
        return at * 2 + which

    ahead = dom_of(place + 1, core)
    behind = dom_of(place - 1, core)
    sibling = me + 1 - 2 * core

    barrier = pltpu.get_barrier_semaphore()
    for other in (ahead, behind, sibling):
        pl.semaphore_signal(barrier, inc=1, device_id={"dom": other}, device_id_type=MESH)

    nodes = feat_ref.shape[0]
    kept = pltpu.make_async_copy(feat_ref, out_ref.at[pl.ds(0, nodes)], local.at[0])
    kept.start()
    depth = min(512, nodes)
    wanted = bound_ref[0:1, :]

    def add_rows(k, total):
        ids = lax.broadcasted_iota(jnp.int32, (depth, ub), 0) + k * depth
        hot = jnp.where(ids == wanted, 1.0, 0.0).astype(BF16)
        rows = feat_ref[pl.ds(pl.multiple_of(k * depth, depth), depth), :]
        return total + lax.dot_general(hot, rows, TN, preferred_element_type=F32)

    total = lax.fori_loop(0, nodes // depth, add_rows, jnp.zeros((ub, width), F32))
    blocks[me, 0:ub, :] = total.astype(BF16)
    blocks[me, ub : ub + n, 0:pick] = pick_ref[...]
    if width > pick:
        blocks[me, ub : ub + n, pick:width] = jnp.zeros((n, width - pick), BF16)
    pl.semaphore_wait(barrier, 3)

    def hop(way, step, h):
        source = place - step if way == 0 else place + step
        owner = dom_of(source, core)
        at = blocks.at[owner, pl.ds(parts[h][0], parts[h][1])]
        return pltpu.make_async_remote_copy(
            src_ref=at,
            dst_ref=at,
            send_sem=send.at[way, step, h],
            recv_sem=recv.at[way, step, h],
            device_id={"dom": ahead if way == 0 else behind},
            device_id_type=MESH,
        )

    def aside(i, owner):
        return pltpu.make_async_remote_copy(
            src_ref=blocks.at[owner],
            dst_ref=blocks.at[owner],
            send_sem=side_send.at[i],
            recv_sem=side_recv.at[i],
            device_id={"dom": sibling},
            device_id_type=MESH,
        )

    def take(owner):
        table = blocks[owner, ub : ub + n, 0:pick].astype(F32)
        rows = lax.broadcasted_iota(jnp.int32, (n, pick), 0)
        mine = jnp.sum(jnp.where(rows == me, table, 0.0), axis=0, keepdims=True)
        ids = lax.broadcasted_iota(jnp.int32, (ub, pick), 0).astype(F32)
        hot = jnp.where(ids == mine, 1.0, 0.0).astype(BF16)
        got = lax.dot_general(hot, blocks[owner, 0:ub, :], TN, preferred_element_type=F32)
        at = pl.ds(pl.multiple_of(nodes + owner * pick, pick), pick)
        out_ref[at, :] = got.astype(BF16)

    started = []
    sides = []
    side_seen = 0

    def arrived(position):
        i = len(sides)
        copy = aside(i, dom_of(position, core))
        copy.start()
        sides.append((copy, position))

    for step in range(full + 1):
        for h in (0, 1):
            for way in (0, 1):
                if step > 0:
                    hop(way, step - 1, h).wait_recv()
                if step < full or h == way:
                    copy = hop(way, step, h)
                    copy.start()
                    started.append(copy)
        if step == 0:
            arrived(place)
            take(me)
        else:
            for position in (place - step, place + step):
                arrived(position)
                take(dom_of(position, core))
            while side_seen < len(sides) - 2:
                copy, position = sides[side_seen]
                copy.wait_recv()
                take(dom_of(position, 1 - core))
                side_seen += 1
    hop(0, full, 0).wait_recv()
    hop(1, full, 1).wait_recv()
    arrived(place + full + 1)
    take(dom_of(place + full + 1, core))
    while side_seen < len(sides):
        copy, position = sides[side_seen]
        copy.wait_recv()
        take(dom_of(position, 1 - core))
        side_seen += 1
    for copy in started:
        copy.wait_send()
    for copy, _ in sides:
        copy.wait_send()
    kept.wait()


def source_rows(n, features, bound_rows, send_pick):
    width = features.shape[1]
    ub = bound_rows.shape[1]
    pick = send_pick.shape[1]
    steps = n // 4
    return pl.pallas_call(
        functools.partial(boundary_kernel, n),
        out_shape=jax.ShapeDtypeStruct((features.shape[0] + n * pick, width), BF16),
        in_specs=[VMEM] * 3,
        out_specs=VMEM,
        scratch_shapes=[
            pltpu.VMEM((n, ub + n, width), BF16),
            pltpu.SemaphoreType.DMA((2, steps, 2)),
            pltpu.SemaphoreType.DMA((2, steps, 2)),
            pltpu.SemaphoreType.DMA((n // 2,)),
            pltpu.SemaphoreType.DMA((n // 2,)),
            pltpu.SemaphoreType.DMA((1,)),
        ],
        compiler_params=pltpu.CompilerParams(
            collective_id=0, has_side_effects=True, vmem_limit_bytes=40 * 2**20
        ),
    )(features, bound_rows, send_pick.astype(BF16))


def tile_kernel(group, dst_ref, src_ref, count_ref, source_ref, tiles_ref, out_ref, total):
    tile = tiles_ref.shape[1]
    total[...] = jnp.zeros_like(total)
    count = count_ref[0]

    def slots(g, carry):
        products = []
        for u in range(group):
            e = g * group + u
            block = source_ref[pl.ds(pl.multiple_of(src_ref[0, e] * tile, tile), tile), :]
            product = jnp.dot(tiles_ref[e], block, preferred_element_type=F32)
            products.append(jnp.where(e < count, product, 0.0))
        for u in range(group):
            e = g * group + u
            at = pl.ds(pl.multiple_of(dst_ref[0, e] * tile, tile), tile)
            total[at, :] += products[u]
        return carry

    lax.fori_loop(0, (count + group - 1) // group, slots, 0)
    out_ref[...] = total[...].astype(BF16)


def aggregate(nodes, source, edge_tiles, tile_dst, tile_src, tile_count):
    width = source.shape[1]
    slots = edge_tiles.shape[0]
    group = next(g for g in (3, 2, 1) if slots % g == 0)
    return pl.pallas_call(
        functools.partial(tile_kernel, group),
        out_shape=jax.ShapeDtypeStruct((nodes, width), BF16),
        in_specs=[SMEM, SMEM, SMEM, VMEM, VMEM],
        out_specs=VMEM,
        scratch_shapes=[pltpu.VMEM((nodes, width), F32)],
        compiler_params=pltpu.CompilerParams(vmem_limit_bytes=30 * 2**20),
    )(tile_dst, tile_src, tile_count, source, edge_tiles)


def halving_plan(n, rows):
    plan = []
    length = rows
    bit = 1
    while bit < n:
        halve = length % 32 == 0
        if halve:
            length //= 2
        plan.append((bit, halve, length))
        bit *= 2
    return plan


def layer_kernel(
    n, nf, plan, chunk, waves,
    feat_ref, agg_ref, ws_ref, wn_ref, bias_ref, cot_ref,
    hidden_ref, gs_ref, gn_ref, gb_ref,
    outgoing, incoming, scales, grads, total, sums, result, halves, small,
    psend, precv, ssend, srecv, gsend, grecv, hsend, hrecv, bsend, brecv, asend, arecv,
):
    me = lax.axis_index("dom")
    f = lax.axis_index("feat")
    owned, units = cot_ref.shape
    width = feat_ref.shape[1]
    chunks = owned // chunk
    lanes = units // waves
    items = waves * chunks
    ahead = min(AHEAD, items)
    lag = min(LAG, chunks)
    span = chunk // 8
    partners = []
    for bit, _, _ in plan:
        side = (me // bit) % 2
        partners.append((me + bit - 2 * bit * side, side))
    joint = len(plan) > 1 and plan[-1][1] and plan[-2][1]
    reach = [partner for partner, _ in partners]
    if joint:
        reach.append(reach[-1] + reach[-2] - me)
    peers = [(f + k) % nf for k in range(1, nf)]

    barrier = pltpu.get_barrier_semaphore()
    for peer in peers:
        pl.semaphore_signal(barrier, inc=1, device_id={"feat": peer}, device_id_type=MESH)
    for partner in reach:
        pl.semaphore_signal(barrier, inc=1, device_id={"dom": partner}, device_id_type=MESH)
    total[...] = jnp.zeros_like(total)
    pl.semaphore_wait(barrier, nf - 1 + len(reach))

    def at_rows(owner, j):
        return pl.ds(pl.multiple_of(owner * owned + j * chunk, chunk), chunk)

    def at_units(w):
        return pl.ds(pl.multiple_of(w * lanes, lanes), lanes)

    def inside(j):
        return pl.ds(pl.multiple_of(j * chunk, chunk), chunk)

    def partial(owner, j, w):
        rows = at_rows(owner, j)
        cols = at_units(w)
        return jnp.dot(feat_ref[rows, :], ws_ref[:, cols], preferred_element_type=F32) + jnp.dot(
            agg_ref[rows, :], wn_ref[:, cols], preferred_element_type=F32
        )

    def push(src, dst, send_sem, recv_sem, axis, to):
        return pltpu.make_async_remote_copy(
            src_ref=src,
            dst_ref=dst,
            send_sem=send_sem,
            recv_sem=recv_sem,
            device_id={axis: to},
            device_id_type=MESH,
        )

    def partial_copy(k, i):
        return push(
            outgoing.at[k, i], incoming.at[k, i], psend.at[k, i], precv.at[k, i], "feat", peers[k]
        )

    def scale_copy(k, i):
        return push(
            scales.at[0, k, i], scales.at[1, k, i], ssend.at[k, i], srecv.at[k, i], "feat", peers[k]
        )

    def grad_copy(k, i):
        at = grads.at[i // chunks, at_rows(f, i % chunks)]
        return push(at, at, gsend.at[k, i], grecv.at[k, i], "feat", peers[k])

    def send_partial(i):
        w, j = i // chunks, i % chunks
        for k in range(nf - 1):
            value = partial(peers[k], j, w).reshape(8, span, lanes)
            top = jnp.max(jnp.max(jnp.abs(value), axis=1), axis=1, keepdims=True)
            top = jnp.broadcast_to(jnp.maximum(top, TINY), (8, lanes))
            scales[0, k, i] = top * (1.0 / LEVELS)
            steps = jnp.round(value * (LEVELS / top)[:, None, :])
            steps = steps.reshape(chunk, lanes).astype(jnp.int32)
            outgoing[k, i] = steps.astype(jnp.int16)
            scale_copy(k, i).start()
            partial_copy(k, i).start()

    def add_grads(owner, i):
        w, j = i // chunks, i % chunks
        rows = at_rows(owner, j)
        block = grads[w, rows, :]
        total[w, 0:width, :] += lax.dot_general(
            feat_ref[rows, :], block, TN, preferred_element_type=F32
        )
        total[w, width : 2 * width, :] += lax.dot_general(
            agg_ref[rows, :], block, TN, preferred_element_type=F32
        )
        wide = block.astype(F32).reshape(chunk // 8, 8, lanes)
        sums[w, owner * chunks + j] = jnp.sum(wide, axis=0)

    def finish(i):
        w, j = i // chunks, i % chunks
        preact = partial(f, j, w)
        cols = at_units(w)
        for k in range(nf - 1):
            scale_copy(k, i).wait_recv()
            partial_copy(k, i).wait_recv()
        for k in range(nf - 1):
            steps = incoming[k, i].astype(jnp.int32).astype(F32)
            value = steps.reshape(8, span, lanes) * scales[1, k, i][:, None, :]
            preact = preact + value.reshape(chunk, lanes)
        preact = preact + bias_ref[:, cols]
        kept = jnp.where(preact > 0.0, cot_ref[inside(j), cols].astype(F32), 0.0)
        grads[w, at_rows(f, j), :] = kept.astype(BF16)
        for k in range(nf - 1):
            grad_copy(k, i).start()
        hidden_ref[inside(j), cols] = jnp.maximum(preact, 0.0).astype(BF16)

    def others(i):
        for k in range(nf - 1):
            grad_copy(k, i).wait_recv()
            add_grads((f + nf - 1 - k) % nf, i)

    def each(low, high, do):
        def step(i, carry):
            do(i)
            return carry

        if high > low:
            lax.fori_loop(low, high, step, 0)

    started = []

    def reduction(w):
        bias_sum = lax.fori_loop(
            0, nf * chunks, lambda i, acc: acc + sums[w, i], jnp.zeros(sums.shape[2:], F32)
        )
        bias_sum = jnp.broadcast_to(jnp.sum(bias_sum, axis=0, keepdims=True), bias_sum.shape)
        base = 0
        bases = []
        for s, (bit, halve, length) in enumerate(plan):
            partner, side = partners[s]
            bases.append(base)
            if halve:
                keep = base + side * length
                give = base + (1 - side) * length
            else:
                keep = give = base
            keep_rows = pl.ds(pl.multiple_of(keep, 16), length)
            give_rows = pl.ds(pl.multiple_of(give, 16), length)
            small[w, 2 * s] = bias_sum
            staged = len(halves[s]) > 1
            if staged:
                halves[s][1][w] = total[w, give_rows, :].astype(halves[s][1].dtype)
            copy = push(
                halves[s][1].at[w] if staged else total.at[w, give_rows],
                halves[s][0].at[w],
                hsend.at[w, s],
                hrecv.at[w, s],
                "dom",
                partner,
            )
            copy.start()
            tiny = push(
                small.at[w, 2 * s], small.at[w, 2 * s + 1], bsend.at[w, s], brecv.at[w, s], "dom", partner
            )
            tiny.start()
            started.extend((copy, tiny))
            yield
            copy.wait_recv()
            total[w, keep_rows, :] += halves[s][0][w].astype(F32)
            tiny.wait_recv()
            bias_sum = bias_sum + small[w, 2 * s + 1]
            base = keep
        last = plan[-1][2]
        rows = pl.ds(pl.multiple_of(base, 16), last)
        result[w, rows, :] = total[w, rows, :].astype(BF16)
        gb_ref[:, w * lanes : (w + 1) * lanes] = bias_sum
        if joint:
            steps = len(plan)
            copies = []
            for slot, partner in ((steps - 1, reach[-2]), (steps - 2, reach[-3]), (steps, reach[-1])):
                at = result.at[w, rows]
                copies.append(push(at, at, asend.at[w, slot], arecv.at[w, slot], "dom", partner))
                copies[-1].start()
            started.extend(copies)
            yield
            for copy in copies:
                copy.wait_recv()
        for s in range(len(plan) - (3 if joint else 1), -1, -1):
            bit, halve, length = plan[s]
            if not halve:
                continue
            partner, side = partners[s]
            at = result.at[w, pl.ds(pl.multiple_of(bases[s] + side * length, 16), length)]
            copy = push(at, at, asend.at[w, s], arecv.at[w, s], "dom", partner)
            copy.start()
            started.append(copy)
            yield
            copy.wait_recv()
        gs_ref[:, w * lanes : (w + 1) * lanes] = result[w, 0:width, :]
        gn_ref[:, w * lanes : (w + 1) * lanes] = result[w, width : 2 * width, :]

    def item(i):
        finish(i)

        @pl.when(i + ahead < items)
        def _():
            send_partial(i + ahead)

        add_grads(f, i)

        @pl.when(i >= lag)
        def _():
            others(i - lag)

    each(0, ahead, send_partial)
    running = [reduction(w) for w in range(waves - 1)]
    first = (waves - 1) * chunks + lag if waves > 1 else items
    each(0, first, item)
    for i in range(first, items):
        running = [r for r in running if next(r, 0) is None]
        item(i)
    for i in range(items - lag, items):
        others(i)
        running = [r for r in running if next(r, 0) is None]
    running = [reduction(waves - 1)] + running
    while running:
        running = [r for r in running if next(r, 0) is None]
    for copy in started:
        copy.wait_send()

    def drain(i):
        for k in range(nf - 1):
            scale_copy(k, i).wait_send()
            partial_copy(k, i).wait_send()
            grad_copy(k, i).wait_send()

    each(0, items, drain)


def layer(n, nf, features, aggregated, w_self, w_neigh, hidden_bias, cotangent):
    nodes, width = features.shape
    owned, units = cotangent.shape
    chunk = min(256, owned)
    chunks = owned // chunk
    waves = 2 if units % 256 == 0 else 1
    lanes = units // waves
    items = waves * chunks
    plan = halving_plan(n, 2 * width)
    halves = []
    for bit, halve, length in plan:
        kind = BF16 if halve and bit > 1 else F32
        one = [pltpu.VMEM((waves, length, lanes), kind)]
        if kind == BF16 or not halve:
            one.append(pltpu.VMEM((waves, length, lanes), kind))
        halves.append(tuple(one))
    steps = len(plan)
    dma = pltpu.SemaphoreType.DMA
    others = max(nf - 1, 1)
    return pl.pallas_call(
        functools.partial(layer_kernel, n, nf, plan, chunk, waves),
        out_shape=(
            jax.ShapeDtypeStruct((owned, units), BF16),
            jax.ShapeDtypeStruct((width, units), BF16),
            jax.ShapeDtypeStruct((width, units), BF16),
            jax.ShapeDtypeStruct((8, units), F32),
        ),
        in_specs=[VMEM] * 6,
        out_specs=(VMEM,) * 4,
        scratch_shapes=[
            pltpu.VMEM((others, items, chunk, lanes), jnp.int16),
            pltpu.VMEM((others, items, chunk, lanes), jnp.int16),
            pltpu.VMEM((2, others, items, 8, lanes), F32),
            pltpu.VMEM((waves, nodes, lanes), BF16),
            pltpu.VMEM((waves, 2 * width, lanes), F32),
            pltpu.VMEM((waves, nf * chunks, 8, lanes), F32),
            pltpu.VMEM((waves, 2 * width, lanes), BF16),
            tuple(halves),
            pltpu.VMEM((waves, 2 * steps, 8, lanes), F32),
        ]
        + [dma((others, items))] * 6
        + [dma((waves, steps + 1))] * 6,
        compiler_params=pltpu.CompilerParams(
            collective_id=1, has_side_effects=True, vmem_limit_bytes=28 * 2**20
        ),
    )(features, aggregated, w_self, w_neigh, hidden_bias[None, :], cotangent)


def body(
    n, nf, features, w_self, w_neigh, hidden_bias, edge_tiles, tile_dst, tile_src, tile_count,
    bound_rows, send_pick, cotangent,
):
    source = source_rows(n, features, bound_rows, send_pick[0])
    aggregated = aggregate(
        features.shape[0], source, edge_tiles[0], tile_dst, tile_src, tile_count
    )
    hidden, grad_self, grad_neigh, grad_bias = layer(
        n, nf, features, aggregated, w_self, w_neigh, hidden_bias, cotangent
    )
    return hidden, grad_self, grad_neigh, grad_bias[0]


def solution(mesh):
    placed = (
        P("dom", "feat"),
        P("feat", None),
        P("feat", None),
        P(),
        P("dom", None, None, None),
        P("dom", None),
        P("dom", None),
        P("dom"),
        P("dom", None),
        P("dom", None, None),
        P(("dom", "feat"), None),
    )
    return jax.shard_map(
        functools.partial(body, mesh.shape["dom"], mesh.shape["feat"]),
        mesh=mesh,
        in_specs=placed,
        out_specs=(P(("dom", "feat"), None), P("feat", None), P("feat", None), P()),
        check_vma=False,
    )
```
